32 devices in a mesh: sec: 2 (over core), req: 4 (over z), head: 4 (over y, x).
Axes of the slice: x: 2, y: 2, z: 4, core: 2. Of those that a mesh axis runs over, the one named last changes fastest.
Arguments:
- queries: bfloat16 [32, 32, 4096], P(('sec', 'req'), None, 'head'), as said below
- tree_keys: bfloat16 [32, 32, 512], P(('sec', 'req'), None, 'head'), may hold values from -4 to 4
- tree_values: bfloat16 [32, 32, 512], P(('sec', 'req'), None, 'head'), may hold values from -4 to 4
- cache_keys: bfloat16 [32, 4, 4096, 128], P(('sec', 'req'), 'head'), as said below
- cache_values: bfloat16 [32, 4, 4096, 128], P(('sec', 'req'), 'head'), may hold values from -4 to 4
- cache_lengths: int32 [32], P(('sec', 'req')), may hold values from 1024 to 4096
- tree_parents: int32 [32, 32], P(('sec', 'req')), may hold values from 0 to 30, as said below
- out_weight: bfloat16 [4096, 2048], P('head'), may hold values from -0.09375 to 0.09375
- hidden: bfloat16 [1024, 2048], P(('sec', 'req', 'head')), may hold values from -0.1796875 to 0.1796875
- norm_gain: float32 [2048], replicated, may hold values from 0.1 to 1.9
- expert_ids: int32 [1024, 8], P(('sec', 'req', 'head')), may hold values from 0 to 31, all different within a row; in each aligned block of 32 rows (0 to 31, 32 to 63, ...) at most 16 rows name the same one
- route_weights: float32 [1024, 8], P(('sec', 'req', 'head')), may hold values from 0.05 to 0.25
- expert_gate_up: bfloat16 [32, 2048, 1536], P(('sec', 'req', 'head')), may hold values from -0.125 to 0.125
- expert_down: bfloat16 [32, 768, 2048], P(('sec', 'req', 'head')), may hold values from -0.21875 to 0.21875
Outputs:
- layer_out: bfloat16 [1024, 2048], P(('sec', 'req', 'head'))
The draws below stay inside these ranges and needn't reach their ends.
Inputs may be any that keep to these rules, and one draw needn't show every extreme that they name: `queries`: values lie within -4.5 to 4.5. `cache_keys`: values lie within -4.5 to 4.5. tree_parents[r, i] < i for i >= 1, and tree_parents[r, 0] = 0. `expert_ids`: each row names 8 different experts. Among the 32 rows of one device (aligned blocks of rows), no expert is named more than 16 times, a bound that some block reaches.
All inputs are finite; a program needn't handle non-finite values.
Results may differ from the reference program's by a relative error of at most 0.02.
Values may be sent and summed in bfloat16 or wider, within the bound.
A program may use at most 128 MiB of HBM per device.

```python
import math
import jax
import jax.numpy as jnp
import numpy as np
from jax import lax

D = 2048
HEADS = 32
KVH = 4
HD = 128
FFE = 768
TOPK = 8
TREE = 32
CACHE = 4096
EXPERTS = 32
REQUESTS = 32
TOKENS = 1024
TOK_SHARD = 32
CAP = 16


def draw_queries(key, part):
    drawn = 1.5 * jax.random.truncated_normal(jax.random.fold_in(key, 21), -3.0, 3.0, (REQUESTS, TREE, KVH, HEADS // KVH, HD), jnp.float32)
    return drawn.reshape(REQUESTS, TREE, HEADS * HD).astype(jnp.bfloat16)


def draw_cache_keys(key, part):
    drawn = jax.random.truncated_normal(jax.random.fold_in(key, 31), -3.0, 3.0, (REQUESTS, KVH, CACHE, HD), jnp.float32)
    return drawn.astype(jnp.bfloat16)


def draw_tree_parents(key, part):
    limits = jnp.maximum(jnp.arange(TREE, dtype=jnp.int32), 1)
    return jax.random.randint(jax.random.fold_in(key, 41), (REQUESTS, TREE), 0, limits[None, :], dtype=jnp.int32)


def touch_ends(result, stream_key, low, largest):
    place = [jax.random.randint(jax.random.fold_in(stream_key, axis), (), 0, length) for axis, length in enumerate(result.shape)]
    longest = result.shape.index(max(result.shape))
    beside = place[:longest] + [(place[longest] + 1) % result.shape[longest]] + place[longest + 1:]
    return result.at[tuple(place)].set(low).at[tuple(beside)].set(largest)


def shard_levels(stream_key, extent, cuts, smallest, high):
    def one(dim, parts):
        draws = jax.random.uniform(jax.random.fold_in(jax.random.fold_in(stream_key, 6), dim), (parts,), jnp.float32, smallest / len(cuts), high / len(cuts))
        return jnp.repeat(jnp.exp(draws), extent[dim] // parts).reshape((-1,) + (1,) * (len(extent) - dim - 1))

    loudness = one(*cuts[0])
    for cut in cuts[1:]:
        loudness = loudness * one(*cut)
    return loudness


def deal_out(own_key, own, number, rows, count, top, bound, skew):
    order = jax.random.permutation(own_key, count)
    crowded, ordinary = portions_of(count, rows * top, bound, skew, True), portions_of(count, rows * top, bound, skew, False)
    places = jnp.arange(count)

    def named(tallies, rotation):
        used = int((tallies > 0).sum())
        fixed = max(1, used // 4)
        moved = fixed + (places - fixed + rotation * (used - fixed)) % max(1, count - fixed)
        return jnp.zeros((count,), jnp.int32).at[order[jnp.where(places < fixed, places, moved)]].set(jnp.asarray(tallies, jnp.int32))

    tallies = jnp.where(number % 4 == 0, named(crowded, number // 4), named(ordinary, number - number // 4 - 1))
    mixed = jax.random.permutation(jax.random.fold_in(own, 3), count)
    source_of, taker = mixed[0:count // 2 * 2:2], mixed[1:count // 2 * 2:2]
    room = jnp.minimum(tallies[source_of] - 1, bound - tallies[taker]) // 2
    room = jnp.where((source_of == order[0]) | (taker == order[0]) | (tallies[taker] == 0), 0, jnp.maximum(room, 0))
    moved = jax.random.randint(jax.random.fold_in(own, 4), (count // 2,), 0, 1 << 20) % (room + 1)
    tallies = tallies.at[source_of].add(-moved).at[taker].add(moved)
    members = jnp.searchsorted(jnp.cumsum(tallies), jnp.arange(rows * top), side="right").astype(jnp.int32)
    grid = members.reshape(top, rows).T
    grid = grid[jax.random.permutation(jax.random.fold_in(own, 1), rows)]
    rotation = jax.random.randint(jax.random.fold_in(own, 2), (rows, 1), 0, top)
    return jnp.take_along_axis(grid, (jnp.arange(top)[None, :] + rotation) % top, axis=1)


def portions_of(number_of, total, reach, skew, full):
    loads = [(1 << 20) // math.isqrt(grade ** skew) + 1 for grade in range(1, number_of + 1)]
    largest = reach if full else min(reach, max(-(-total // number_of), total * loads[0] // sum(loads)))
    least = 1 if total - largest >= number_of - 1 else 0
    given, rest = [largest] + [least] * (number_of - 1), total - largest - least * (number_of - 1)
    while rest > 0:
        movable = [i for i in range(1, number_of) if given[i] < largest] or [i for i in range(1, number_of) if given[i] < reach]
        whole, budget = sum([loads[i] for i in movable]), rest
        for i in movable:
            extra = min(reach - given[i], max(1, budget * loads[i] // whole), rest)
            given[i] = given[i] + extra
            rest = rest - extra
    return np.array(given)


def scatter_about(own_key, dims, deviation, reach, cuts=(), kind=jnp.bfloat16):
    array = jax.random.normal(own_key, dims, jnp.float32) * deviation
    if len(cuts) > 0:
        array = shard_levels(own_key, dims, cuts, -0.22, 0.18) * array
    return jnp.clip(array, min=-reach, max=reach).astype(kind)


def setup_inputs(seed: int = 0) -> dict:
    splits = jax.random.split(jax.random.key(seed), 15)
    queries = draw_queries(jax.random.fold_in(splits[14], 71), 0)
    tree_keys = scatter_about(splits[1], (REQUESTS, TREE, KVH * HD), 1.0, 4.0, ((0, 8), (2, 4)))
    tree_values = scatter_about(splits[2], (REQUESTS, TREE, KVH * HD), 1.0, 4.0, ((0, 8), (2, 4)))
    cache_keys = draw_cache_keys(jax.random.fold_in(splits[14], 71), 0)
    cache_values = scatter_about(splits[4], (REQUESTS, KVH, CACHE, HD), 1.0, 4.0, ((0, 8), (1, 4)))
    cache_lengths = touch_ends(jax.random.randint(splits[5], (REQUESTS,), CACHE // 4, CACHE + 1), jax.random.fold_in(splits[5], 1), CACHE // 4, CACHE).astype(jnp.int32)
    tree_parents = draw_tree_parents(jax.random.fold_in(splits[14], 71), 0)
    out_weight = scatter_about(splits[7], (HEADS * HD, D), (HEADS * HD) ** -0.5, 0.09375, ((0, 4),))
    hidden = scatter_about(splits[8], (TOKENS, D), 0.03, 0.1796875, ((0, 32),))
    norm_gain = jnp.clip(1.0 + 0.18 * jax.random.normal(splits[9], (D,), jnp.float32), 0.1, 1.9)
    expert_ids_keys = jax.random.split(jax.random.fold_in(splits[10], 1), TOKENS // TOK_SHARD)
    expert_ids_turns = jax.random.permutation(jax.random.fold_in(splits[10], 3), TOKENS // TOK_SHARD)
    expert_ids = jax.vmap(lambda own, number: deal_out(jax.random.fold_in(splits[10], 2), own, number, TOK_SHARD, EXPERTS, TOPK, CAP, 2))(expert_ids_keys, expert_ids_turns).reshape((TOKENS, TOPK))
    route_weights = jnp.clip(0.05 + 0.2 * jax.random.uniform(splits[11], (TOKENS, TOPK), jnp.float32) ** shard_levels(splits[11], (TOKENS, TOPK), ((0, 32),), -0.2, 0.2), 0.05, 0.25)
    expert_gate_up = scatter_about(splits[12], (EXPERTS, D, 2 * FFE), D ** -0.5, 0.125, ((0, 32),))
    expert_down = scatter_about(splits[13], (EXPERTS, FFE, D), FFE ** -0.5, 0.21875, ((0, 32),))
    return {"queries": queries, "tree_keys": tree_keys, "tree_values": tree_values, "cache_keys": cache_keys, "cache_values": cache_values, "cache_lengths": cache_lengths, "tree_parents": tree_parents, "out_weight": out_weight, "hidden": hidden, "norm_gain": norm_gain, "expert_ids": expert_ids, "route_weights": route_weights, "expert_gate_up": expert_gate_up, "expert_down": expert_down}


def ancestors(parents):
    length = parents.shape[-1]
    labels = jnp.arange(length, dtype=jnp.int32)
    linked = (parents[..., :, None] == labels).astype(jnp.float32)
    closure = jnp.minimum(linked + jnp.eye(length, dtype=jnp.float32), 1.0)
    for repeat in range(max(1, (length - 1).bit_length())):
        closure = jnp.minimum(jnp.einsum('rij,rjk->rik', closure, closure), 1.0)
    return closure

def attend_request(packed):
    query_rows, tree_keys, tree_values, cache_keys, cache_values, cache_length, closure = packed
    tree_len = query_rows.shape[0]
    kv_heads, cache_len, head_dim = cache_keys.shape
    groups = query_rows.shape[1] // (kv_heads * head_dim)
    query_split = query_rows.astype(jnp.float32).reshape(tree_len, kv_heads, groups, head_dim)
    tree_keyed = tree_keys.astype(jnp.float32).reshape(tree_len, kv_heads, head_dim)
    tree_valued = tree_values.astype(jnp.float32).reshape(tree_len, kv_heads, head_dim)
    score_scale = head_dim ** (-0.5)
    cache_scores = jnp.einsum('skgd,kcd->kgsc', query_split, cache_keys.astype(jnp.float32)) * score_scale
    tree_scores = jnp.einsum('skgd,tkd->kgst', query_split, tree_keyed) * score_scale
    cache_valid = jnp.arange(cache_len, dtype=jnp.int32) < cache_length
    cache_scores = jnp.where(cache_valid, cache_scores, -1e+30)
    tree_scores = jnp.where(closure > 0.5, tree_scores, -1e+30)
    highest = jnp.maximum(lax.optimization_barrier(jnp.max(cache_scores, -1)), lax.optimization_barrier(jnp.max(tree_scores, -1)))[..., None]
    cache_exp = jnp.exp(cache_scores - highest)
    tree_exp = jnp.exp(tree_scores - highest)
    denominator = lax.optimization_barrier(jnp.sum(cache_exp, -1, keepdims=True)) + lax.optimization_barrier(jnp.sum(tree_exp, -1, keepdims=True))
    cache_prob = lax.optimization_barrier((cache_exp / denominator).astype(jnp.bfloat16)).astype(jnp.float32)
    tree_prob = lax.optimization_barrier((tree_exp / denominator).astype(jnp.bfloat16)).astype(jnp.float32)
    attended = jnp.einsum('kgsc,kcd->skgd', cache_prob, cache_values.astype(jnp.float32))
    attended = attended + jnp.einsum('kgst,tkd->skgd', tree_prob, tree_valued)
    return attended.reshape(tree_len, query_rows.shape[1]).astype(jnp.bfloat16)

def expert_apply(packed):
    expert_rows, gate_up, down_proj = packed
    mixed = jnp.dot(expert_rows, gate_up, preferred_element_type=jnp.float32)
    activated = (jax.nn.silu(mixed[:, :FFE]) * mixed[:, FFE:]).astype(jnp.bfloat16)
    return jnp.dot(activated, down_proj, preferred_element_type=jnp.float32).astype(jnp.bfloat16)

def reference(queries, tree_keys, tree_values, cache_keys, cache_values, cache_lengths, tree_parents, out_weight, hidden, norm_gain, expert_ids, route_weights, expert_gate_up, expert_down):
    closure = ancestors(tree_parents)
    attended = lax.map(attend_request, (queries, tree_keys, tree_values, cache_keys, cache_values, cache_lengths, closure))
    attended = attended.reshape(TOKENS, HEADS * HD)
    resid = hidden.astype(jnp.float32) + jnp.dot(attended, out_weight, preferred_element_type=jnp.float32)
    normed = (resid * lax.rsqrt(lax.optimization_barrier(jnp.mean(resid * resid, -1, keepdims=True)) + 1e-06) * norm_gain).astype(jnp.bfloat16)
    flat_ids = expert_ids.reshape(-1).astype(jnp.int32)
    bucket_size = TOKENS // TOK_SHARD * CAP
    onehot = (flat_ids[:, None] == jnp.arange(EXPERTS, dtype=jnp.int32)[None, :]).astype(jnp.int32)
    ranking = lax.optimization_barrier(jnp.sum((jnp.cumsum(onehot, 0) - onehot) * onehot, -1)).astype(jnp.int32)
    slot_index = (flat_ids * bucket_size + ranking).astype(jnp.int32)
    owners = (jnp.arange(TOKENS * TOPK, dtype=jnp.int32) // TOPK).astype(jnp.int32)
    token_of = jnp.zeros((EXPERTS * bucket_size,), jnp.int32).at[slot_index].set(owners)
    expert_rows = normed[token_of].reshape(EXPERTS, bucket_size, D)
    outputs = lax.map(expert_apply, (expert_rows, expert_gate_up, expert_down)).reshape(EXPERTS * bucket_size, D)
    picked = outputs[slot_index].reshape(TOKENS, TOPK, D).astype(jnp.float32)
    expert_sum = jnp.einsum('tk,tkd->td', route_weights, picked)
    return (resid + expert_sum).astype(jnp.bfloat16)
```

```python
import functools
import math

import jax
import jax.numpy as jnp
from jax import lax
from jax.experimental import pallas as pl
from jax.experimental.pallas import tpu as pltpu
from jax.sharding import PartitionSpec as P

F32 = jnp.float32
BF16 = jnp.bfloat16
NEG = -1e30
CHUNK = 2048
LANES = 128


def dot_nt(a, b):
    return lax.dot_general(a, b, (((1,), (1,)), ((), ())), preferred_element_type=F32)


def dot_nn(a, b):
    return jnp.dot(a, b, preferred_element_type=F32)


def copy_count(z_n, y_n, x_n):
    gather = 2 * (z_n - 1) + z_n * (x_n * y_n - 1) * 2 + 2 * z_n * y_n * x_n
    back = 2 * z_n + 2 * z_n * (y_n - 1 + x_n - 1) + 2 * (z_n - 1)
    route = (z_n - 1) + (y_n * x_n - 1) + 1
    return (y_n * x_n - 1) + gather + back + route


def closures(par_ref):
    n, tree = par_ref.shape
    down = lax.broadcasted_iota(jnp.int32, (tree, tree), 0)
    across = lax.broadcasted_iota(jnp.int32, (tree, tree), 1)
    eye = (down == across).astype(F32)
    result = []
    for r in range(n):
        linked_t = (jnp.broadcast_to(par_ref[r : r + 1, :], (tree, tree)) == down).astype(F32)
        linked = dot_nt(eye.astype(BF16), linked_t.astype(BF16))
        result.append(jnp.minimum(linked + eye, 1.0))
    for _ in range(max(1, (tree - 1).bit_length())):
        result = [jnp.minimum(dot_nn(c.astype(BF16), c.astype(BF16)), 1.0) for c in result]
    return result


def layer_kernel(
    dims, len_ref, q_ref, tk_ref, tv_ref, par_ref, hid_ref, gain_ref, ids_ref, rw_ref,
    ck_hbm, cv_hbm, wo_hbm, gu_hbm, dn_hbm, out_ref,
    kbuf, vbuf, wide, closed, attended, part_out, head_in, routes,
    bank, sums, pair_in, first_in, second_in, z_in, resid_ref, gu,
    send, recv, load_sem, kv_sem,
):
    z_n, y_n, x_n = dims
    h_n = y_n * x_n
    s = lax.axis_index("sec")
    z = lax.axis_index("req")
    h = lax.axis_index("head")
    y = h // x_n
    x = h % x_n
    tok, model = hid_ref.shape
    half = model // 2
    mine = (s * z_n + z) * h_n + h

    def to_head(k):
        return {"head": lax.rem(h + k, h_n)}

    def to_z(k):
        return {"req": lax.rem(z + k, z_n)}

    def to_yx(dy, dx):
        return {"head": lax.rem(y + dy, y_n) * x_n + lax.rem(x + dx, x_n)}

    partner = {"sec": 1 - s}
    barrier = pltpu.get_barrier_semaphore()
    peers = [to_head(k) for k in range(1, h_n)] + [to_z(k) for k in range(1, z_n)] + [partner]
    for peer in peers:
        pl.semaphore_signal(
            barrier, inc=1, device_id=peer, device_id_type=pl.DeviceIdType.MESH
        )

    reqs, tree, width = q_ref.shape
    assert reqs == h_n and tree == tok
    which = [lax.rem(h + k, h_n) for k in range(1, h_n + 1)]
    load_k = [
        pltpu.make_async_copy(ck_hbm.at[which[k], 0], kbuf.at[k % 2], kv_sem.at[0, k])
        for k in range(reqs)
    ]
    load_v = [
        pltpu.make_async_copy(cv_hbm.at[which[k], 0], vbuf.at[k % 2], kv_sem.at[1, k])
        for k in range(reqs)
    ]
    load_wo = pltpu.make_async_copy(wo_hbm, wide.at[pl.ds(0, width)], load_sem.at[2])
    load_gu = pltpu.make_async_copy(gu_hbm.at[0], gu, load_sem.at[0])
    ffe = dn_hbm.shape[1]
    load_dn = pltpu.make_async_copy(dn_hbm.at[0], wide.at[pl.ds(0, ffe)], load_sem.at[1])
    for k in range(2):
        load_k[k].start()
        load_v[k].start()
    load_wo.start()
    load_gu.start()

    made = []

    def push(src, dst, peer):
        k = len(made)
        c = pltpu.make_async_remote_copy(
            src_ref=src, dst_ref=dst, send_sem=send.at[k], recv_sem=recv.at[k],
            device_id=peer, device_id_type=pl.DeviceIdType.MESH,
        )
        made.append(c)
        c.start()
        return c

    lanes = routes.shape[-1]
    labels = lax.broadcasted_iota(jnp.int32, (lanes, tok), 0)
    dense = jnp.zeros((lanes, tok), F32)
    for k in range(ids_ref.shape[0]):
        dense = dense + jnp.where(ids_ref[k : k + 1, :] == labels, rw_ref[k : k + 1, :], 0.0)
    routes[0, 0, 0] = dense.T

    for r, c in enumerate(closures(par_ref)):
        closed[r] = c

    cache, hd = ck_hbm.shape[2:]
    groups = width // hd
    scale = hd ** (-0.5) * math.log2(math.e)
    chunks = cache // CHUNK
    assert cache % CHUNK == 0
    state = {}

    def rows_of(k):
        q = q_ref[which[k]]
        rows = jnp.concatenate([q[:, g * hd : (g + 1) * hd] for g in range(groups)], axis=0)
        return (rows.astype(F32) * scale).astype(BF16)

    def score(k, c):
        if c == 0:
            state[k] = rows_of(k)
        sc = dot_nt(state[k], kbuf[k % 2, c * CHUNK : (c + 1) * CHUNK])
        place = lax.broadcasted_iota(jnp.int32, (1, CHUNK), 1)
        return sc + jnp.where(place < len_ref[which[k]] - c * CHUNK, 0.0, NEG)

    def project(ks):
        a = attended[ks[0] : ks[-1] + 1].reshape(len(ks) * tree, width)
        return dot_nn(a, wide[:width])

    arrivals = []

    def send_part(ks):
        out = project(ks).astype(BF16)
        for i, k in enumerate(ks):
            part_out[k] = out[i * tok : (i + 1) * tok]
        for k in ks:
            arrivals.append(push(part_out.at[k], head_in.at[k], to_head(k + 1)))

    route_z, route_h = [], []

    def after(k):
        if k == 1:
            load_wo.wait()
            pl.semaphore_wait(barrier, len(peers))
            for dz in range(1, z_n):
                route_z.append(push(routes.at[0, 0, 0], routes.at[0, 0, dz], to_z(dz)))
            send_part([0, 1])
        elif k == h_n - 2:
            send_part([k])
            for c in route_z:
                c.wait_recv()
            for j in range(1, h_n):
                route_h.append(
                    push(routes.at[0, 0], routes.at[0, j], to_yx(j // x_n, j % x_n))
                )

    load_k[0].wait()
    load_v[0].wait()
    steps = [(k, c) for k in range(reqs) for c in range(chunks)]
    ahead = score(0, 0)
    for i, (k, c) in enumerate(steps):
        now_s = ahead
        if c == chunks - 1 and k + 1 < reqs:
            load_k[k + 1].wait()
            load_v[k + 1].wait()
        if i + 1 < len(steps):
            ahead = score(*steps[i + 1])
        if c == 0:
            admitted = jnp.concatenate([closed[which[k]]] * groups, axis=0)
            st = jnp.where(admitted > 0.5, dot_nt(state[k], tk_ref[which[k]]), NEG)
            m = jnp.max(st, -1, keepdims=True)
            p = jnp.exp2(st - m)
            l = jnp.sum(p, -1, keepdims=True)
            acc = dot_nn(p.astype(BF16), tv_ref[which[k]])
        now = jnp.maximum(m, jnp.max(now_s, -1, keepdims=True))
        p = jnp.exp2(now_s - now)
        fade = jnp.exp2(m - now)
        l = l * fade + jnp.sum(p, -1, keepdims=True)
        acc = acc * fade + dot_nn(p.astype(BF16), vbuf[k % 2, c * CHUNK : (c + 1) * CHUNK])
        m = now
        if c == chunks - 1:
            o = (acc / l).astype(BF16)
            for g in range(groups):
                attended[k, :, g * hd : (g + 1) * hd] = o[g * tree : (g + 1) * tree]
            if k + 2 < reqs:
                load_k[k + 2].start()
                load_v[k + 2].start()
            after(k)

    resid = hid_ref[...].astype(F32) + project([reqs - 1])
    load_dn.start()
    for k in range(h_n - 1):
        arrivals[k].wait_recv()
        resid = resid + head_in[k].astype(F32)
    resid_ref[...] = resid
    normed = (
        resid * lax.rsqrt(jnp.mean(resid * resid, -1, keepdims=True) + 1e-06) * gain_ref[...]
    ).astype(BF16)
    for f in range(2):
        bank[0, f, 0, 0, 0] = normed[:, f * half : (f + 1) * half]
    got = {}

    def gather(f, dz, dy, dx, src, peer):
        got[f, dz, dy, dx] = push(
            bank.at[(0, f, dz) + src], bank.at[0, f, dz, dy, dx], peer
        )

    for dz in range(1, z_n):
        for f in range(2):
            got[f, dz, 0, 0] = push(bank.at[0, f, 0, 0, 0], bank.at[0, f, dz, 0, 0], to_z(dz))

    crossed = {}

    def cross(f, dz, dy, dx):
        crossed[f, dz, dy, dx] = push(
            bank.at[0, f, dz, dy, dx], bank.at[1, f, dz, dy, dx], partner
        )

    def stage_a(dz):
        for f in range(2):
            if dz:
                got[f, dz, 0, 0].wait_recv()
            cross(f, dz, 0, 0)
            for dx in range(1, x_n):
                gather(f, dz, 0, dx, (0, 0), to_yx(0, dx)) if f == 0 else None
            for dy in range(1, y_n):
                gather(f, dz, dy, 0, (0, 0), to_yx(dy, 0)) if f == 1 else None
        for dy in range(1, y_n):
            gather(0, dz, dy, 0, (0, 0), to_yx(dy, 0))
        for dx in range(1, x_n):
            gather(1, dz, 0, dx, (0, 0), to_yx(0, dx))

    def stage_b(dz):
        for dx in range(1, x_n):
            got[0, dz, 0, dx].wait_recv()
            for dy in range(1, y_n):
                gather(0, dz, dy, dx, (0, dx), to_yx(dy, 0))
            cross(0, dz, 0, dx)
        for dy in range(1, y_n):
            got[1, dz, dy, 0].wait_recv()
            for dx in range(1, x_n):
                gather(1, dz, dy, dx, (dy, 0), to_yx(0, dx))
            cross(1, dz, dy, 0)

    def stage_c(dz):
        for f in range(2):
            for dy in range(y_n):
                for dx in range(x_n):
                    seen = (dy == 0 and dx == 0) or (f == 0 and dy == 0) or (f == 1 and dx == 0)
                    if not seen:
                        got[f, dz, dy, dx].wait_recv()
                        cross(f, dz, dy, dx)

    count = 2 * h_n * tok
    apart = 1 if h_n * tok <= 128 else y_n

    def experts(dz):
        for f in range(2):
            for dy in range(y_n):
                for dx in range(x_n):
                    crossed[f, dz, dy, dx].wait_recv()
        pick = lax.broadcasted_iota(jnp.int32, (1, lanes), 1) == mine
        for part in range(apart):
            ys = slice(part * (y_n // apart), (part + 1) * (y_n // apart))
            left = bank[:, 0, dz, ys].reshape(count // apart, half)
            right = bank[:, 1, dz, ys].reshape(count // apart, half)
            hs = slice(ys.start * x_n, ys.stop * x_n)
            named = routes[:, hs, dz].reshape(count // apart, lanes)
            weight = jnp.sum(jnp.where(pick, named, 0.0), -1, keepdims=True)
            mixed = dot_nn(left, gu[:half]) + dot_nn(right, gu[half:])
            hidden = mixed.shape[1] // 2
            gate = mixed[:, :hidden]
            active = (gate / (1.0 + jnp.exp(-gate)) * mixed[:, hidden:]).astype(BF16)
            result = jnp.where(weight > 0.0, dot_nn(active, wide[:ffe]) * weight, 0.0).astype(BF16)
            shaped = result.reshape(2, y_n // apart, x_n, tok, model)
            for f in range(2):
                sums[f, dz, ys] = shaped[0, ..., f * half : (f + 1) * half]
                bank[1, f, dz, ys] = shaped[1, ..., f * half : (f + 1) * half]

    paired, firsts, seconds, ends = {}, {}, {}, {}

    def back_pair(dz):
        for f in range(2):
            paired[f, dz] = push(
                bank.at[1, f, dz], pair_in.at[f, dz], partner
            )

    def back_first(dz):
        for f in range(2):
            paired[f, dz].wait_recv()
            sums[f, dz] = (sums[f, dz].astype(F32) + pair_in[f, dz].astype(F32)).astype(BF16)
            if f == 0:
                for dy in range(1, y_n):
                    firsts[f, dz, dy] = push(
                        sums.at[f, dz, dy], first_in.at[f, dz, dy - 1], to_yx(y_n - dy, 0)
                    )
            else:
                for dx in range(1, x_n):
                    firsts[f, dz, dx] = push(
                        sums.at[f, dz, :, dx], first_in.at[f, dz, dx - 1], to_yx(0, x_n - dx)
                    )

    def back_second(dz):
        for f in range(2):
            total = sums[f, dz, 0] if f == 0 else sums[f, dz, :, 0]
            total = total.astype(F32)
            for d in range(1, y_n if f == 0 else x_n):
                firsts[f, dz, d].wait_recv()
                total = total + first_in[f, dz, d - 1].astype(F32)
            if f == 0:
                sums[f, dz, 0] = total.astype(BF16)
                for dx in range(1, x_n):
                    seconds[f, dz, dx] = push(
                        sums.at[f, dz, 0, dx], second_in.at[f, dz, dx - 1], to_yx(0, x_n - dx)
                    )
            else:
                sums[f, dz, :, 0] = total.astype(BF16)
                for dy in range(1, y_n):
                    seconds[f, dz, dy] = push(
                        sums.at[f, dz, dy, 0], second_in.at[f, dz, dy - 1], to_yx(y_n - dy, 0)
                    )

    def back_end(dz):
        for f in range(2):
            total = sums[f, dz, 0, 0].astype(F32)
            for d in range(1, x_n if f == 0 else y_n):
                seconds[f, dz, d].wait_recv()
                total = total + second_in[f, dz, d - 1].astype(F32)
            if dz:
                sums[f, dz, 0, 0] = total.astype(BF16)
                ends[f, dz] = push(sums.at[f, dz, 0, 0], z_in.at[f, dz - 1], to_z(z_n - dz))
            else:
                cols = slice(f * half, (f + 1) * half)
                resid_ref[:, cols] = resid_ref[:, cols] + total

    order = list(range(1, z_n)) + [0]

    def back(j):
        for stage, lag in ((back_end, 3), (back_second, 2), (back_first, 1)):
            if 0 <= j - lag < z_n:
                stage(order[j - lag])

    ran = 0
    for i in range(z_n + 2):
        for stage, lag in ((stage_a, 0), (stage_b, 1), (stage_c, 2)):
            if 0 <= i - lag < z_n:
                stage(i - lag)
        if i == 1:
            for c in route_h:
                c.wait_recv()
            crossed_routes = push(routes.at[0], routes.at[1], partner)
        if i == 2:
            load_gu.wait()
            load_dn.wait()
            crossed_routes.wait_recv()
        while ran < z_n and (i == z_n + 1 or order[ran] <= i - 2 and order[ran] > 0):
            experts(order[ran])
            back_pair(order[ran])
            back(ran)
            ran += 1
    for j in range(z_n, z_n + 3):
        back(j)
    for f in range(2):
        cols = slice(f * half, (f + 1) * half)
        total = resid_ref[:, cols]
        for dz in range(1, z_n):
            ends[f, dz].wait_recv()
            total = total + z_in[f, dz - 1].astype(F32)
        out_ref[:, cols] = total.astype(BF16)
    for c in made:
        c.wait_send()
    assert len(made) == copy_count(*dims)


def layer(dims, q, tk, tv, ck, cv, lengths, parents, out_weight, hidden, gain, ids, route, gate_up,
          down):
    z_n, y_n, x_n = dims
    tok, model = hidden.shape
    half = model // 2
    h_n = y_n * x_n
    reqs, tree, width = q.shape
    cache, hd = ck.shape[2:]
    experts = gate_up.shape[0] * 2 * z_n * h_n
    assert gate_up.shape[0] == 1 and ck.shape[1] == 1
    lanes = -(-experts // LANES) * LANES
    most = max(y_n, x_n)
    copies = copy_count(*dims)
    vmem = pl.BlockSpec(memory_space=pltpu.VMEM)
    return pl.pallas_call(
        functools.partial(layer_kernel, dims),
        out_shape=jax.ShapeDtypeStruct((tok, model), BF16),
        in_specs=[pl.BlockSpec(memory_space=pltpu.SMEM)] + [vmem] * 8
        + [pl.BlockSpec(memory_space=pl.ANY)] * 5,
        out_specs=vmem,
        scratch_shapes=[
            pltpu.VMEM((2, cache, hd), BF16),
            pltpu.VMEM((2, cache, hd), BF16),
            pltpu.VMEM((max(width, down.shape[1]), model), BF16),
            pltpu.VMEM((reqs, tree, tree), F32),
            pltpu.VMEM((reqs, tree, width), BF16),
            pltpu.VMEM((h_n - 1, tok, model), BF16),
            pltpu.VMEM((h_n - 1, tok, model), BF16),
            pltpu.VMEM((2, h_n, z_n, tok, lanes), F32),
            pltpu.VMEM((2, 2, z_n, y_n, x_n, tok, half), BF16),
            pltpu.VMEM((2, z_n, y_n, x_n, tok, half), BF16),
            pltpu.VMEM((2, z_n, y_n, x_n, tok, half), BF16),
            pltpu.VMEM((2, z_n, most - 1, most, tok, half), BF16),
            pltpu.VMEM((2, z_n, most - 1, tok, half), BF16),
            pltpu.VMEM((2, z_n - 1, tok, half), BF16),
            pltpu.VMEM((tok, model), F32),
            pltpu.VMEM(gate_up.shape[1:], BF16),
            pltpu.SemaphoreType.DMA((copies,)),
            pltpu.SemaphoreType.DMA((copies,)),
            pltpu.SemaphoreType.DMA((3,)),
            pltpu.SemaphoreType.DMA((2, reqs)),
        ],
        compiler_params=pltpu.CompilerParams(
            collective_id=0, has_side_effects=True, vmem_limit_bytes=67043328
        ),
    )(lengths, q, tk, tv, parents, hidden, gain.reshape(1, -1), ids.T, route.T, ck, cv,
      out_weight, gate_up, down)


def per_device(
    dims, queries, tree_keys, tree_values, cache_keys, cache_values, cache_lengths, tree_parents,
    out_weight, hidden, norm_gain, expert_ids, route_weights, expert_gate_up, expert_down,
):
    return layer(
        dims, queries, tree_keys, tree_values, cache_keys, cache_values, cache_lengths,
        tree_parents, out_weight, hidden, norm_gain, expert_ids, route_weights, expert_gate_up,
        expert_down,
    )


def solution(mesh):
    heads = mesh.shape["head"]
    x_n = math.isqrt(heads)
    while heads % x_n:
        x_n -= 1
    assert mesh.shape["sec"] == 2
    dims = (mesh.shape["req"], heads // x_n, x_n)
    tokens = ("sec", "req", "head")
    in_specs = (
        P(("sec", "req"), None, "head"),
        P(("sec", "req"), None, "head"),
        P(("sec", "req"), None, "head"),
        P(("sec", "req"), "head", None, None),
        P(("sec", "req"), "head", None, None),
        P(("sec", "req")),
        P(("sec", "req"), None),
        P("head", None),
        P(tokens, None),
        P(),
        P(tokens, None),
        P(tokens, None),
        P(tokens, None, None),
        P(tokens, None, None),
    )
    return jax.shard_map(
        functools.partial(per_device, dims), mesh=mesh, in_specs=in_specs,
        out_specs=P(tokens, None), check_vma=False,
    )
```

```python
import functools
import math

import jax
import jax.numpy as jnp
from jax import lax
from jax.experimental import pallas as pl
from jax.experimental.pallas import tpu as pltpu
from jax.sharding import PartitionSpec as P

F32 = jnp.float32
BF16 = jnp.bfloat16
NEG = -1e30
CHUNK = 2048
LANES = 128


def dot_nt(a, b):
    return lax.dot_general(a, b, (((1,), (1,)), ((), ())), preferred_element_type=F32)


def dot_nn(a, b):
    return jnp.dot(a, b, preferred_element_type=F32)


def copy_count(z_n, y_n, x_n):
    gather = 2 * (z_n - 1) + z_n * (x_n * y_n - 1) * 2 + 2 * z_n * y_n * x_n
    back = 2 * z_n + 2 * z_n * (y_n - 1 + x_n - 1) + 2 * (z_n - 1)
    route = (z_n - 1) + (y_n * x_n - 1) + 1
    return (y_n * x_n - 1) + gather + back + route


def closures(par_ref):
    n, tree = par_ref.shape
    down = lax.broadcasted_iota(jnp.int32, (tree, tree), 0)
    across = lax.broadcasted_iota(jnp.int32, (tree, tree), 1)
    eye = (down == across).astype(F32)
    result = []
    for r in range(n):
        linked_t = (jnp.broadcast_to(par_ref[r : r + 1, :], (tree, tree)) == down).astype(F32)
        linked = dot_nt(eye.astype(BF16), linked_t.astype(BF16))
        result.append(jnp.minimum(linked + eye, 1.0))
    for _ in range(max(1, (tree - 1).bit_length())):
        result = [jnp.minimum(dot_nn(c.astype(BF16), c.astype(BF16)), 1.0) for c in result]
    return result


def layer_kernel(
    dims, len_ref, q_ref, tk_ref, tv_ref, par_ref, hid_ref, gain_ref, ids_ref, rw_ref,
    ck_hbm, cv_hbm, wo_hbm, gu_hbm, dn_hbm, out_ref,
    kbuf, vbuf, wide, closed, attended, part_out, head_in, routes,
    bank, active, sums, pair_in, first_in, second_in, z_in, resid_ref, gu,
    send, recv, load_sem, kv_sem,
):
    z_n, y_n, x_n = dims
    h_n = y_n * x_n
    s = lax.axis_index("sec")
    z = lax.axis_index("req")
    h = lax.axis_index("head")
    y = h // x_n
    x = h % x_n
    tok, model = hid_ref.shape
    half = model // 2
    mine = (s * z_n + z) * h_n + h

    def to_head(k):
        return {"head": lax.rem(h + k, h_n)}

    def to_z(d):
        other = z
        for bit in range(z_n.bit_length()):
            if d >> bit & 1:
                other = other + 2**bit - 2 ** (bit + 1) * lax.rem(z // 2**bit, 2)
        return {"req": other}

    def to_yx(dy, dx):
        return {"head": lax.rem(y + dy, y_n) * x_n + lax.rem(x + dx, x_n)}

    partner = {"sec": 1 - s}
    barrier = pltpu.get_barrier_semaphore()
    peers = [to_head(k) for k in range(1, h_n)] + [to_z(k) for k in range(1, z_n)] + [partner]
    for peer in peers:
        pl.semaphore_signal(
            barrier, inc=1, device_id=peer, device_id_type=pl.DeviceIdType.MESH
        )

    reqs, tree, width = q_ref.shape
    assert reqs == h_n and tree == tok and z_n & (z_n - 1) == 0
    which = [lax.rem(h + k, h_n) for k in range(1, h_n + 1)]
    load_k = [
        pltpu.make_async_copy(ck_hbm.at[which[k], 0], kbuf.at[k % 2], kv_sem.at[0, k])
        for k in range(reqs)
    ]
    load_v = [
        pltpu.make_async_copy(cv_hbm.at[which[k], 0], vbuf.at[k % 2], kv_sem.at[1, k])
        for k in range(reqs)
    ]
    load_wo = pltpu.make_async_copy(wo_hbm, wide.at[pl.ds(0, width)], load_sem.at[2])
    load_gu = pltpu.make_async_copy(gu_hbm.at[0], gu, load_sem.at[0])
    ffe = dn_hbm.shape[1]
    load_dn = pltpu.make_async_copy(dn_hbm.at[0], wide.at[pl.ds(0, ffe)], load_sem.at[1])
    load_k[0].start()
    load_v[0].start()

    made = []

    def push(src, dst, peer):
        k = len(made)
        c = pltpu.make_async_remote_copy(
            src_ref=src, dst_ref=dst, send_sem=send.at[k], recv_sem=recv.at[k],
            device_id=peer, device_id_type=pl.DeviceIdType.MESH,
        )
        made.append(c)
        c.start()
        return c

    lanes = routes.shape[-1]
    labels = lax.broadcasted_iota(jnp.int32, (lanes, tok), 0)
    dense = jnp.zeros((lanes, tok), F32)
    for k in range(ids_ref.shape[0]):
        dense = dense + jnp.where(ids_ref[k : k + 1, :] == labels, rw_ref[k : k + 1, :], 0.0)
    routes[0, 0, 0] = dense.T

    for r, c in enumerate(closures(par_ref)):
        closed[r] = c

    cache, hd = ck_hbm.shape[2:]
    groups = width // hd
    scale = hd ** (-0.5) * math.log2(math.e)
    chunks = cache // CHUNK
    assert cache % CHUNK == 0
    state = {}

    def rows_of(k):
        q = q_ref[which[k]]
        rows = jnp.concatenate([q[:, g * hd : (g + 1) * hd] for g in range(groups)], axis=0)
        return (rows.astype(F32) * scale).astype(BF16)

    def score(k, c):
        if c == 0:
            state[k] = rows_of(k)
        sc = dot_nt(state[k], kbuf[k % 2, c * CHUNK : (c + 1) * CHUNK])
        place = lax.broadcasted_iota(jnp.int32, (1, CHUNK), 1)
        return sc + jnp.where(place < len_ref[which[k]] - c * CHUNK, 0.0, NEG)

    def project(ks):
        a = attended[ks[0] : ks[-1] + 1].reshape(len(ks) * tree, width)
        return dot_nn(a, wide[:width])

    arrivals = []

    def send_part(ks):
        out = project(ks).astype(BF16)
        for i, k in enumerate(ks):
            part_out[k] = out[i * tok : (i + 1) * tok]
        for k in ks:
            arrivals.append(push(part_out.at[k], head_in.at[k], to_head(k + 1)))

    route_z, route_h, route_s = [], [], []

    def after(k):
        if k == 0:
            for c in route_z:
                c.wait_recv()
            for j in range(1, h_n):
                route_h.append(
                    push(routes.at[0, 0], routes.at[0, j], to_yx(j // x_n, j % x_n))
                )
        elif k == 1:
            load_wo.wait()
            load_gu.start()
            send_part([0, 1])
        elif k == h_n - 2:
            send_part([k])
            for c in route_h:
                c.wait_recv()
            route_s.append(push(routes.at[0], routes.at[1], partner))

    pl.semaphore_wait(barrier, len(peers))
    for d in range(1, z_n):
        route_z.append(push(routes.at[0, 0, 0], routes.at[0, 0, d], to_z(d)))
    load_k[0].wait()
    load_v[0].wait()
    load_k[1].start()
    load_v[1].start()
    load_wo.start()
    steps = [(k, c) for k in range(reqs) for c in range(chunks)]
    ahead = score(0, 0)
    for i, (k, c) in enumerate(steps):
        now_s = ahead
        if c == chunks - 1 and k + 1 < reqs:
            load_k[k + 1].wait()
            load_v[k + 1].wait()
        if i + 1 < len(steps):
            ahead = score(*steps[i + 1])
        if c == 0:
            admitted = jnp.concatenate([closed[which[k]]] * groups, axis=0)
            st = jnp.where(admitted > 0.5, dot_nt(state[k], tk_ref[which[k]]), NEG)
            m = jnp.max(st, -1, keepdims=True)
            p = jnp.exp2(st - m)
            l = jnp.sum(p, -1, keepdims=True)
            acc = dot_nn(p.astype(BF16), tv_ref[which[k]])
        now = jnp.maximum(m, jnp.max(now_s, -1, keepdims=True))
        p = jnp.exp2(now_s - now)
        fade = jnp.exp2(m - now)
        l = l * fade + jnp.sum(p, -1, keepdims=True)
        acc = acc * fade + dot_nn(p.astype(BF16), vbuf[k % 2, c * CHUNK : (c + 1) * CHUNK])
        m = now
        if c == chunks - 1:
            o = (acc / l).astype(BF16)
            for g in range(groups):
                attended[k, :, g * hd : (g + 1) * hd] = o[g * tree : (g + 1) * tree]
            if k + 2 < reqs:
                load_k[k + 2].start()
                load_v[k + 2].start()
            after(k)

    resid = hid_ref[...].astype(F32) + project([reqs - 1])
    load_dn.start()
    for k in range(h_n - 1):
        arrivals[k].wait_recv()
        resid = resid + head_in[k].astype(F32)
    resid_ref[...] = resid
    normed = (
        resid * lax.rsqrt(jnp.mean(resid * resid, -1, keepdims=True) + 1e-06) * gain_ref[...]
    ).astype(BF16)
    for f in range(2):
        bank[0, f, 0, 0, 0] = normed[:, f * half : (f + 1) * half]
    got, crossed = {}, {}

    def gather(f, d, dy, dx, src, peer):
        got[f, d, dy, dx] = push(bank.at[(0, f, d) + src], bank.at[0, f, d, dy, dx], peer)

    def cross(f, d, dy, dx):
        crossed[f, d, dy, dx] = push(
            bank.at[0, f, d, dy, dx], bank.at[1, f, d, dy, dx], partner
        )

    def stage_a(d):
        if d:
            for f in range(2):
                got[f, d, 0, 0].wait_recv()
                for low in [2**b for b in range((d & -d).bit_length() - 1)]:
                    got[f, d + low, 0, 0] = push(
                        bank.at[0, f, d, 0, 0], bank.at[0, f, d + low, 0, 0], to_z(low)
                    )
        for dx in range(1, x_n):
            gather(0, d, 0, dx, (0, 0), to_yx(0, dx))
        for dy in range(1, y_n):
            gather(1, d, dy, 0, (0, 0), to_yx(dy, 0))
        for dy in range(1, y_n):
            gather(0, d, dy, 0, (0, 0), to_yx(dy, 0))
        for dx in range(1, x_n):
            gather(1, d, 0, dx, (0, 0), to_yx(0, dx))
        for f in range(2):
            cross(f, d, 0, 0)

    def stage_b(d):
        for dx in range(1, x_n):
            got[0, d, 0, dx].wait_recv()
            for dy in range(1, y_n):
                gather(0, d, dy, dx, (0, dx), to_yx(dy, 0))
        for dy in range(1, y_n):
            got[1, d, dy, 0].wait_recv()
            for dx in range(1, x_n):
                gather(1, d, dy, dx, (dy, 0), to_yx(0, dx))
        for dx in range(1, x_n):
            cross(0, d, 0, dx)
        for dy in range(1, y_n):
            cross(1, d, dy, 0)

    def stage_c(d):
        late = [(0, dy, 0) for dy in range(1, y_n)] + [(1, 0, dx) for dx in range(1, x_n)]
        late += [(f, dy, dx) for f in range(2) for dy in range(1, y_n) for dx in range(1, x_n)]
        for f, dy, dx in late:
            got[f, d, dy, dx].wait_recv()
            cross(f, d, dy, dx)

    rows = 2 * h_n * tok
    hidden = gu.shape[1] // 2
    step = hidden // 3
    paired, firsts, seconds, ends = {}, {}, {}, {}

    def compute(d, hooks):
        for c in [crossed[f, d, dy, dx] for f in range(2) for dy in range(y_n) for dx in range(x_n)]:
            c.wait_recv()
        left = bank[:, 0, d].reshape(rows, half)
        right = bank[:, 1, d].reshape(rows, half)
        for j in range(3):
            cols = slice(j * step, (j + 1) * step)
            ups = slice(hidden + j * step, hidden + (j + 1) * step)
            gate = dot_nn(left, gu[:half, cols]) + dot_nn(right, gu[half:, cols])
            up = dot_nn(left, gu[:half, ups]) + dot_nn(right, gu[half:, ups])
            active[:, cols] = (gate / (1.0 + jnp.exp(-gate)) * up).astype(BF16)
            hooks[j]()
        pick = lax.broadcasted_iota(jnp.int32, (1, lanes), 1) == mine
        named = routes[:, :, d].reshape(rows, lanes)
        weight = jnp.sum(jnp.where(pick, named, 0.0), -1, keepdims=True)
        for f in range(2):
            result = dot_nn(active[...], wide[:ffe, f * half : (f + 1) * half]) * weight
            shaped = result.astype(BF16).reshape(2, y_n, x_n, tok, half)
            sums[f, d] = shaped[0]
            bank[1, f, d] = shaped[1]
            paired[f, d] = push(bank.at[1, f, d], pair_in.at[f, d], partner)
            hooks[3 + f]()

    def back_first(d):
        for f in range(2):
            paired[f, d].wait_recv()
            sums[f, d] = (sums[f, d].astype(F32) + pair_in[f, d].astype(F32)).astype(BF16)
            if f == 0:
                for dy in range(1, y_n):
                    firsts[f, d, dy] = push(
                        sums.at[f, d, dy], first_in.at[f, d, dy - 1], to_yx(y_n - dy, 0)
                    )
            else:
                for dx in range(1, x_n):
                    firsts[f, d, dx] = push(
                        sums.at[f, d, :, dx], first_in.at[f, d, dx - 1], to_yx(0, x_n - dx)
                    )

    def back_second(d):
        for f in range(2):
            total = sums[f, d, 0] if f == 0 else sums[f, d, :, 0]
            total = total.astype(F32)
            for k in range(1, y_n if f == 0 else x_n):
                firsts[f, d, k].wait_recv()
                total = total + first_in[f, d, k - 1].astype(F32)
            if f == 0:
                sums[f, d, 0] = total.astype(BF16)
                for dx in range(1, x_n):
                    seconds[f, d, dx] = push(
                        sums.at[f, d, 0, dx], second_in.at[f, d, dx - 1], to_yx(0, x_n - dx)
                    )
            else:
                sums[f, d, :, 0] = total.astype(BF16)
                for dy in range(1, y_n):
                    seconds[f, d, dy] = push(
                        sums.at[f, d, dy, 0], second_in.at[f, d, dy - 1], to_yx(y_n - dy, 0)
                    )

    def back_end(d):
        for f in range(2):
            total = sums[f, d, 0, 0].astype(F32)
            for k in range(1, x_n if f == 0 else y_n):
                seconds[f, d, k].wait_recv()
                total = total + second_in[f, d, k - 1].astype(F32)
            if d:
                sums[f, d, 0, 0] = total.astype(BF16)
                ends[f, d] = push(sums.at[f, d, 0, 0], z_in.at[f, d - 1], to_z(d))
            else:
                cols = slice(f * half, (f + 1) * half)
                resid_ref[:, cols] = resid_ref[:, cols] + total

    done = set()

    def run(*stages):
        for stage, d in stages:
            if 0 <= d < z_n and (stage, d) not in done:
                done.add((stage, d))
                stage(d)

    for d in [2**b for b in range(z_n.bit_length() - 1)]:
        for f in range(2):
            got[f, d, 0, 0] = push(bank.at[0, f, 0, 0, 0], bank.at[0, f, d, 0, 0], to_z(d))
    run((stage_a, 0), (stage_b, 0), (stage_a, 1))
    run((stage_c, 0))
    load_gu.wait()
    load_dn.wait()
    route_s[0].wait_recv()
    n = z_n - 1
    for i in range(z_n):
        compute(i, [
            lambda: run((stage_b, i + 1)),
            lambda: run((back_first, i - 1 or -1)),
            lambda: run((stage_a, i + 2)),
            lambda: run((back_second, i - 2 or -1)),
            lambda: run((stage_c, i + 1), (back_end, i - 3 or -1)),
        ])
    run((back_first, n), (back_end, n - 2), (back_second, n - 1), (back_second, n))
    run((back_first, 0), (back_end, n - 1), (back_end, n), (back_second, 0), (back_end, 0))
    for f in range(2):
        cols = slice(f * half, (f + 1) * half)
        total = resid_ref[:, cols]
        for d in range(1, z_n):
            ends[f, d].wait_recv()
            total = total + z_in[f, d - 1].astype(F32)
        out_ref[:, cols] = total.astype(BF16)
    for c in made:
        c.wait_send()
    assert len(made) == copy_count(*dims)


def layer(dims, q, tk, tv, ck, cv, lengths, parents, out_weight, hidden, gain, ids, route, gate_up,
          down):
    z_n, y_n, x_n = dims
    tok, model = hidden.shape
    half = model // 2
    h_n = y_n * x_n
    reqs, tree, width = q.shape
    cache, hd = ck.shape[2:]
    experts = gate_up.shape[0] * 2 * z_n * h_n
    assert gate_up.shape[0] == 1 and ck.shape[1] == 1
    lanes = -(-experts // LANES) * LANES
    most = max(y_n, x_n)
    copies = copy_count(*dims)
    vmem = pl.BlockSpec(memory_space=pltpu.VMEM)
    return pl.pallas_call(
        functools.partial(layer_kernel, dims),
        out_shape=jax.ShapeDtypeStruct((tok, model), BF16),
        in_specs=[pl.BlockSpec(memory_space=pltpu.SMEM)] + [vmem] * 8
        + [pl.BlockSpec(memory_space=pl.ANY)] * 5,
        out_specs=vmem,
        scratch_shapes=[
            pltpu.VMEM((2, cache, hd), BF16),
            pltpu.VMEM((2, cache, hd), BF16),
            pltpu.VMEM((max(width, down.shape[1]), model), BF16),
            pltpu.VMEM((reqs, tree, tree), F32),
            pltpu.VMEM((reqs, tree, width), BF16),
            pltpu.VMEM((h_n - 1, tok, model), BF16),
            pltpu.VMEM((h_n - 1, tok, model), BF16),
            pltpu.VMEM((2, h_n, z_n, tok, lanes), F32),
            pltpu.VMEM((2, 2, z_n, y_n, x_n, tok, half), BF16),
            pltpu.VMEM((2 * h_n * tok, down.shape[1]), BF16),
            pltpu.VMEM((2, z_n, y_n, x_n, tok, half), BF16),
            pltpu.VMEM((2, z_n, y_n, x_n, tok, half), BF16),
            pltpu.VMEM((2, z_n, most - 1, most, tok, half), BF16),
            pltpu.VMEM((2, z_n, most - 1, tok, half), BF16),
            pltpu.VMEM((2, z_n - 1, tok, half), BF16),
            pltpu.VMEM((tok, model), F32),
            pltpu.VMEM(gate_up.shape[1:], BF16),
            pltpu.SemaphoreType.DMA((copies,)),
            pltpu.SemaphoreType.DMA((copies,)),
            pltpu.SemaphoreType.DMA((3,)),
            pltpu.SemaphoreType.DMA((2, reqs)),
        ],
        compiler_params=pltpu.CompilerParams(
            collective_id=0, has_side_effects=True, vmem_limit_bytes=67043328
        ),
    )(lengths, q, tk, tv, parents, hidden, gain.reshape(1, -1), ids.T, route.T, ck, cv,
      out_weight, gate_up, down)


def per_device(
    dims, queries, tree_keys, tree_values, cache_keys, cache_values, cache_lengths, tree_parents,
    out_weight, hidden, norm_gain, expert_ids, route_weights, expert_gate_up, expert_down,
):
    return layer(
        dims, queries, tree_keys, tree_values, cache_keys, cache_values, cache_lengths,
        tree_parents, out_weight, hidden, norm_gain, expert_ids, route_weights, expert_gate_up,
        expert_down,
    )


def solution(mesh):
    heads = mesh.shape["head"]
    x_n = math.isqrt(heads)
    while heads % x_n:
        x_n -= 1
    assert mesh.shape["sec"] == 2
    dims = (mesh.shape["req"], heads // x_n, x_n)
    tokens = ("sec", "req", "head")
    in_specs = (
        P(("sec", "req"), None, "head"),
        P(("sec", "req"), None, "head"),
        P(("sec", "req"), None, "head"),
        P(("sec", "req"), "head", None, None),
        P(("sec", "req"), "head", None, None),
        P(("sec", "req")),
        P(("sec", "req"), None),
        P("head", None),
        P(tokens, None),
        P(),
        P(tokens, None),
        P(tokens, None),
        P(tokens, None, None),
        P(tokens, None, None),
    )
    return jax.shard_map(
        functools.partial(per_device, dims), mesh=mesh, in_specs=in_specs,
        out_specs=P(tokens, None), check_vma=False,
    )
```

```python
import functools
import math

import jax
import jax.numpy as jnp
from jax import lax
from jax.experimental import pallas as pl
from jax.experimental.pallas import tpu as pltpu
from jax.sharding import PartitionSpec as P

F32 = jnp.float32
BF16 = jnp.bfloat16
NEG = -1e30
CHUNK = 1024
LANES = 128


def dot_nt(a, b):
    return lax.dot_general(a, b, (((1,), (1,)), ((), ())), preferred_element_type=F32)


def dot_nn(a, b):
    return jnp.dot(a, b, preferred_element_type=F32)


def copy_count(z_n, y_n, x_n):
    gather = 2 * (z_n - 1) + z_n * (x_n * y_n - 1) * 2 + 2 * z_n * y_n * x_n
    back = 2 * z_n + 2 * z_n * (y_n - 1 + x_n - 1) + 2 * (z_n - 1)
    route = (z_n - 1) + (y_n * x_n - 1) + 1
    return (y_n * x_n - 1) + gather + back + route


def closures(par_ref):
    n, tree = par_ref.shape
    down = lax.broadcasted_iota(jnp.int32, (tree, tree), 0)
    across = lax.broadcasted_iota(jnp.int32, (tree, tree), 1)
    eye = (down == across).astype(F32)
    result = []
    for r in range(n):
        linked_t = (jnp.broadcast_to(par_ref[r : r + 1, :], (tree, tree)) == down).astype(F32)
        linked = dot_nt(eye.astype(BF16), linked_t.astype(BF16))
        result.append(jnp.minimum(linked + eye, 1.0))
    for _ in range(max(1, (tree - 1).bit_length())):
        result = [jnp.minimum(dot_nn(c.astype(BF16), c.astype(BF16)), 1.0) for c in result]
    return result


def layer_kernel(
    dims, len_ref, q_ref, tk_ref, tv_ref, par_ref, hid_ref, gain_ref, ids_ref, rw_ref,
    ck_hbm, cv_hbm, wo_hbm, gu_hbm, dn_hbm, out_ref,
    kbuf, vbuf, wide, closed, attended, part_out, head_in, routes,
    bank, active, sums, pair_in, first_in, second_in, z_in, resid_ref, gu,
    send, recv, load_sem, kv_sem,
):
    z_n, y_n, x_n = dims
    h_n = y_n * x_n
    s = lax.axis_index("sec")
    z = lax.axis_index("req")
    h = lax.axis_index("head")
    y = h // x_n
    x = h % x_n
    tok, model = hid_ref.shape
    half = model // 2
    mine = (s * z_n + z) * h_n + h

    def to_head(k):
        return {"head": lax.rem(h + k, h_n)}

    def to_z(d):
        other = z
        for bit in range(z_n.bit_length()):
            if d >> bit & 1:
                other = other + 2**bit - 2 ** (bit + 1) * lax.rem(z // 2**bit, 2)
        return {"req": other}

    def to_yx(dy, dx):
        return {"head": lax.rem(y + dy, y_n) * x_n + lax.rem(x + dx, x_n)}

    partner = {"sec": 1 - s}
    barrier = pltpu.get_barrier_semaphore()
    peers = [to_head(k) for k in range(1, h_n)] + [to_z(k) for k in range(1, z_n)] + [partner]
    for peer in peers:
        pl.semaphore_signal(
            barrier, inc=1, device_id=peer, device_id_type=pl.DeviceIdType.MESH
        )

    reqs, tree, width = q_ref.shape
    assert reqs == h_n and tree == tok and z_n & (z_n - 1) == 0
    away = [divmod(k, x_n) for k in reversed(range(h_n))]
    which = [to_yx(*a)["head"] for a in away]
    load_k = [
        pltpu.make_async_copy(ck_hbm.at[which[k], 0], kbuf.at[k % 2], kv_sem.at[0, k])
        for k in range(reqs)
    ]
    load_v = [
        pltpu.make_async_copy(cv_hbm.at[which[k], 0], vbuf.at[k % 2], kv_sem.at[1, k])
        for k in range(reqs)
    ]
    load_wo = pltpu.make_async_copy(wo_hbm, wide.at[pl.ds(0, width)], load_sem.at[2])
    load_gu = pltpu.make_async_copy(gu_hbm.at[0], gu, load_sem.at[0])
    ffe = dn_hbm.shape[1]
    load_dn = pltpu.make_async_copy(dn_hbm.at[0], wide.at[pl.ds(0, ffe)], load_sem.at[1])
    load_k[0].start()
    load_v[0].start()

    made = []

    def push(src, dst, peer):
        k = len(made)
        c = pltpu.make_async_remote_copy(
            src_ref=src, dst_ref=dst, send_sem=send.at[k], recv_sem=recv.at[k],
            device_id=peer, device_id_type=pl.DeviceIdType.MESH,
        )
        made.append(c)
        c.start()
        return c

    lanes = routes.shape[-1]
    labels = lax.broadcasted_iota(jnp.int32, (lanes, tok), 0)
    dense = jnp.zeros((lanes, tok), F32)
    for k in range(ids_ref.shape[0]):
        dense = dense + jnp.where(ids_ref[k : k + 1, :] == labels, rw_ref[k : k + 1, :], 0.0)
    routes[0, 0, 0] = dense.T

    for r, c in enumerate(closures(par_ref)):
        closed[r] = c

    cache, hd = ck_hbm.shape[2:]
    groups = width // hd
    scale = hd ** (-0.5) * math.log2(math.e)
    chunks = cache // CHUNK
    assert cache % CHUNK == 0
    state = {}

    def rows_of(k):
        q = q_ref[which[k]]
        rows = jnp.concatenate([q[:, g * hd : (g + 1) * hd] for g in range(groups)], axis=0)
        return (rows.astype(F32) * scale).astype(BF16)

    def score(k, c):
        if c == 0:
            state[k] = rows_of(k)
        sc = dot_nt(state[k], kbuf[k % 2, c * CHUNK : (c + 1) * CHUNK])
        place = lax.broadcasted_iota(jnp.int32, (1, CHUNK), 1)
        return sc + jnp.where(place < len_ref[which[k]] - c * CHUNK, 0.0, NEG)

    def project(ks):
        a = attended[ks[0] : ks[-1] + 1].reshape(len(ks) * tree, width)
        return dot_nn(a, wide[:width])

    arrivals = []

    def send_part(ks):
        out = project(ks).astype(BF16)
        for i, k in enumerate(ks):
            part_out[k] = out[i * tok : (i + 1) * tok]
        for k in ks:
            arrivals.append(push(part_out.at[k], head_in.at[k], to_yx(*away[k])))

    route_z, route_h, route_s = [], [], []

    def after(k):
        if k == 0:
            for c in route_z:
                c.wait_recv()
            for j in range(1, h_n):
                route_h.append(
                    push(routes.at[0, 0], routes.at[0, j], to_yx(j // x_n, j % x_n))
                )
        elif k == 1:
            load_wo.wait()
            load_gu.start()
            send_part([0, 1])
        elif k == h_n - 2:
            send_part([k])
            for c in route_h:
                c.wait_recv()
            route_s.append(push(routes.at[0], routes.at[1], partner))

    pl.semaphore_wait(barrier, len(peers))
    for d in range(1, z_n):
        route_z.append(push(routes.at[0, 0, 0], routes.at[0, 0, d], to_z(d)))
    load_k[0].wait()
    load_v[0].wait()
    load_k[1].start()
    load_v[1].start()
    load_wo.start()
    steps = [(k, c) for k in range(reqs) for c in range(chunks)]
    ahead = score(0, 0)
    for i, (k, c) in enumerate(steps):
        now_s = ahead
        if c == chunks - 1 and k + 1 < reqs:
            load_k[k + 1].wait()
            load_v[k + 1].wait()
        if i + 1 < len(steps):
            ahead = score(*steps[i + 1])
        if c == 0:
            admitted = jnp.concatenate([closed[which[k]]] * groups, axis=0)
            st = jnp.where(admitted > 0.5, dot_nt(state[k], tk_ref[which[k]]), NEG)
            m = jnp.max(st, -1, keepdims=True)
            p = jnp.exp2(st - m)
            l = jnp.sum(p, -1, keepdims=True)
            acc = dot_nn(p.astype(BF16), tv_ref[which[k]])
        now = jnp.maximum(m, jnp.max(now_s, -1, keepdims=True))
        p = jnp.exp2(now_s - now)
        fade = jnp.exp2(m - now)
        l = l * fade + jnp.sum(p, -1, keepdims=True)
        acc = acc * fade + dot_nn(p.astype(BF16), vbuf[k % 2, c * CHUNK : (c + 1) * CHUNK])
        m = now
        if c == chunks - 1:
            o = (acc / l).astype(BF16)
            for g in range(groups):
                attended[k, :, g * hd : (g + 1) * hd] = o[g * tree : (g + 1) * tree]
            if k + 2 < reqs:
                load_k[k + 2].start()
                load_v[k + 2].start()
            after(k)

    resid = hid_ref[...].astype(F32) + project([reqs - 1])
    load_dn.start()
    for k in range(h_n - 1):
        arrivals[k].wait_recv()
        resid = resid + head_in[k].astype(F32)
    resid_ref[...] = resid
    normed = (
        resid * lax.rsqrt(jnp.mean(resid * resid, -1, keepdims=True) + 1e-06) * gain_ref[...]
    ).astype(BF16)
    for f in range(2):
        bank[0, f, 0, 0, 0] = normed[:, f * half : (f + 1) * half]
    got, crossed = {}, {}

    def gather(f, d, dy, dx, src, peer):
        got[f, d, dy, dx] = push(bank.at[(0, f, d) + src], bank.at[0, f, d, dy, dx], peer)

    def cross(f, d, dy, dx):
        crossed[f, d, dy, dx] = push(
            bank.at[0, f, d, dy, dx], bank.at[1, f, d, dy, dx], partner
        )

    def stage_a(d):
        if d:
            for f in range(2):
                got[f, d, 0, 0].wait_recv()
                for low in [2**b for b in range((d & -d).bit_length() - 1)]:
                    got[f, d + low, 0, 0] = push(
                        bank.at[0, f, d, 0, 0], bank.at[0, f, d + low, 0, 0], to_z(low)
                    )
        for dx in range(1, x_n):
            gather(0, d, 0, dx, (0, 0), to_yx(0, dx))
        for dy in range(1, y_n):
            gather(1, d, dy, 0, (0, 0), to_yx(dy, 0))
        for dy in range(1, y_n):
            gather(0, d, dy, 0, (0, 0), to_yx(dy, 0))
        for dx in range(1, x_n):
            gather(1, d, 0, dx, (0, 0), to_yx(0, dx))
        for f in range(2):
            cross(f, d, 0, 0)

    def stage_b(d):
        for dx in range(1, x_n):
            got[0, d, 0, dx].wait_recv()
            for dy in range(1, y_n):
                gather(0, d, dy, dx, (0, dx), to_yx(dy, 0))
        for dy in range(1, y_n):
            got[1, d, dy, 0].wait_recv()
            for dx in range(1, x_n):
                gather(1, d, dy, dx, (dy, 0), to_yx(0, dx))
        for dx in range(1, x_n):
            cross(0, d, 0, dx)
        for dy in range(1, y_n):
            cross(1, d, dy, 0)

    def stage_c(d):
        late = [(0, dy, 0) for dy in range(1, y_n)] + [(1, 0, dx) for dx in range(1, x_n)]
        late += [(f, dy, dx) for f in range(2) for dy in range(1, y_n) for dx in range(1, x_n)]
        for f, dy, dx in late:
            got[f, d, dy, dx].wait_recv()
            cross(f, d, dy, dx)

    rows = 2 * h_n * tok
    hidden = gu.shape[1] // 2
    step = hidden // 3
    paired, firsts, seconds, ends = {}, {}, {}, {}

    def compute(d, hooks):
        for c in [crossed[f, d, dy, dx] for f in range(2) for dy in range(y_n) for dx in range(x_n)]:
            c.wait_recv()
        left = bank[:, 0, d].reshape(rows, half)
        right = bank[:, 1, d].reshape(rows, half)
        for j in range(3):
            cols = slice(j * step, (j + 1) * step)
            ups = slice(hidden + j * step, hidden + (j + 1) * step)
            gate = dot_nn(left, gu[:half, cols]) + dot_nn(right, gu[half:, cols])
            up = dot_nn(left, gu[:half, ups]) + dot_nn(right, gu[half:, ups])
            active[:, cols] = (gate / (1.0 + jnp.exp(-gate)) * up).astype(BF16)
            hooks[j]()
        pick = lax.broadcasted_iota(jnp.int32, (1, lanes), 1) == mine
        named = routes[:, :, d].reshape(rows, lanes)
        weight = jnp.sum(jnp.where(pick, named, 0.0), -1, keepdims=True)
        for f in range(2):
            result = dot_nn(active[...], wide[:ffe, f * half : (f + 1) * half]) * weight
            shaped = result.astype(BF16).reshape(2, y_n, x_n, tok, half)
            sums[f, d] = shaped[0]
            bank[1, f, d] = shaped[1]
            paired[f, d] = push(bank.at[1, f, d], pair_in.at[f, d], partner)
            hooks[3 + f]()

    def back_first(d):
        for f in range(2):
            paired[f, d].wait_recv()
            sums[f, d] = (sums[f, d].astype(F32) + pair_in[f, d].astype(F32)).astype(BF16)
            if f == 0:
                for dy in range(1, y_n):
                    firsts[f, d, dy] = push(
                        sums.at[f, d, dy], first_in.at[f, d, dy - 1], to_yx(y_n - dy, 0)
                    )
            else:
                for dx in range(1, x_n):
                    firsts[f, d, dx] = push(
                        sums.at[f, d, :, dx], first_in.at[f, d, dx - 1], to_yx(0, x_n - dx)
                    )

    def back_second(d):
        for f in range(2):
            total = sums[f, d, 0] if f == 0 else sums[f, d, :, 0]
            total = total.astype(F32)
            for k in range(1, y_n if f == 0 else x_n):
                firsts[f, d, k].wait_recv()
                total = total + first_in[f, d, k - 1].astype(F32)
            if f == 0:
                sums[f, d, 0] = total.astype(BF16)
                for dx in range(1, x_n):
                    seconds[f, d, dx] = push(
                        sums.at[f, d, 0, dx], second_in.at[f, d, dx - 1], to_yx(0, x_n - dx)
                    )
            else:
                sums[f, d, :, 0] = total.astype(BF16)
                for dy in range(1, y_n):
                    seconds[f, d, dy] = push(
                        sums.at[f, d, dy, 0], second_in.at[f, d, dy - 1], to_yx(y_n - dy, 0)
                    )

    def back_end(d):
        for f in range(2):
            total = sums[f, d, 0, 0].astype(F32)
            for k in range(1, x_n if f == 0 else y_n):
                seconds[f, d, k].wait_recv()
                total = total + second_in[f, d, k - 1].astype(F32)
            if d:
                sums[f, d, 0, 0] = total.astype(BF16)
                ends[f, d] = push(sums.at[f, d, 0, 0], z_in.at[f, d - 1], to_z(d))
            else:
                cols = slice(f * half, (f + 1) * half)
                resid_ref[:, cols] = resid_ref[:, cols] + total

    done = set()

    def run(*stages):
        for stage, d in stages:
            if 0 <= d < z_n and (stage, d) not in done:
                done.add((stage, d))
                stage(d)

    for d in [2**b for b in range(z_n.bit_length() - 1)]:
        for f in range(2):
            got[f, d, 0, 0] = push(bank.at[0, f, 0, 0, 0], bank.at[0, f, d, 0, 0], to_z(d))
    run((stage_a, 0), (stage_b, 0), (stage_a, 1), (stage_c, 0), (stage_a, 2))
    load_gu.wait()
    load_dn.wait()
    route_s[0].wait_recv()
    n = z_n - 1
    for i in range(z_n):
        compute(i, [
            lambda: run((stage_b, i + 1)),
            lambda: run((back_first, i - 1 or -1)),
            lambda: run((stage_a, i + 3)),
            lambda: run((stage_b, i + 2), (back_second, i - 2 or -1)),
            lambda: run((stage_c, i + 1), (back_end, i - 3 or -1)),
        ])
    run((back_first, n), (back_end, n - 2), (back_second, n - 1), (back_second, n))
    run((back_first, 0), (back_end, n - 1), (back_end, n), (back_second, 0), (back_end, 0))
    for f in range(2):
        cols = slice(f * half, (f + 1) * half)
        total = resid_ref[:, cols]
        for d in range(1, z_n):
            ends[f, d].wait_recv()
            total = total + z_in[f, d - 1].astype(F32)
        out_ref[:, cols] = total.astype(BF16)
    for c in made:
        c.wait_send()
    assert len(made) == copy_count(*dims)


def layer(dims, q, tk, tv, ck, cv, lengths, parents, out_weight, hidden, gain, ids, route, gate_up,
          down):
    z_n, y_n, x_n = dims
    tok, model = hidden.shape
    half = model // 2
    h_n = y_n * x_n
    reqs, tree, width = q.shape
    cache, hd = ck.shape[2:]
    experts = gate_up.shape[0] * 2 * z_n * h_n
    assert gate_up.shape[0] == 1 and ck.shape[1] == 1
    lanes = -(-experts // LANES) * LANES
    most = max(y_n, x_n)
    copies = copy_count(*dims)
    vmem = pl.BlockSpec(memory_space=pltpu.VMEM)
    return pl.pallas_call(
        functools.partial(layer_kernel, dims),
        out_shape=jax.ShapeDtypeStruct((tok, model), BF16),
        in_specs=[pl.BlockSpec(memory_space=pltpu.SMEM)] + [vmem] * 8
        + [pl.BlockSpec(memory_space=pl.ANY)] * 5,
        out_specs=vmem,
        scratch_shapes=[
            pltpu.VMEM((2, cache, hd), BF16),
            pltpu.VMEM((2, cache, hd), BF16),
            pltpu.VMEM((max(width, down.shape[1]), model), BF16),
            pltpu.VMEM((reqs, tree, tree), F32),
            pltpu.VMEM((reqs, tree, width), BF16),
            pltpu.VMEM((h_n - 1, tok, model), BF16),
            pltpu.VMEM((h_n - 1, tok, model), BF16),
            pltpu.VMEM((2, h_n, z_n, tok, lanes), F32),
            pltpu.VMEM((2, 2, z_n, y_n, x_n, tok, half), BF16),
            pltpu.VMEM((2 * h_n * tok, down.shape[1]), BF16),
            pltpu.VMEM((2, z_n, y_n, x_n, tok, half), BF16),
            pltpu.VMEM((2, z_n, y_n, x_n, tok, half), BF16),
            pltpu.VMEM((2, z_n, most - 1, most, tok, half), BF16),
            pltpu.VMEM((2, z_n, most - 1, tok, half), BF16),
            pltpu.VMEM((2, z_n - 1, tok, half), BF16),
            pltpu.VMEM((tok, model), F32),
            pltpu.VMEM(gate_up.shape[1:], BF16),
            pltpu.SemaphoreType.DMA((copies,)),
            pltpu.SemaphoreType.DMA((copies,)),
            pltpu.SemaphoreType.DMA((3,)),
            pltpu.SemaphoreType.DMA((2, reqs)),
        ],
        compiler_params=pltpu.CompilerParams(
            collective_id=0, has_side_effects=True, vmem_limit_bytes=67043328
        ),
    )(lengths, q, tk, tv, parents, hidden, gain.reshape(1, -1), ids.T, route.T, ck, cv,
      out_weight, gate_up, down)


def per_device(
    dims, queries, tree_keys, tree_values, cache_keys, cache_values, cache_lengths, tree_parents,
    out_weight, hidden, norm_gain, expert_ids, route_weights, expert_gate_up, expert_down,
):
    return layer(
        dims, queries, tree_keys, tree_values, cache_keys, cache_values, cache_lengths,
        tree_parents, out_weight, hidden, norm_gain, expert_ids, route_weights, expert_gate_up,
        expert_down,
    )


def solution(mesh):
    heads = mesh.shape["head"]
    x_n = math.isqrt(heads)
    while heads % x_n:
        x_n -= 1
    assert mesh.shape["sec"] == 2
    dims = (mesh.shape["req"], heads // x_n, x_n)
    tokens = ("sec", "req", "head")
    in_specs = (
        P(("sec", "req"), None, "head"),
        P(("sec", "req"), None, "head"),
        P(("sec", "req"), None, "head"),
        P(("sec", "req"), "head", None, None),
        P(("sec", "req"), "head", None, None),
        P(("sec", "req")),
        P(("sec", "req"), None),
        P("head", None),
        P(tokens, None),
        P(),
        P(tokens, None),
        P(tokens, None),
        P(tokens, None, None),
        P(tokens, None, None),
    )
    return jax.shard_map(
        functools.partial(per_device, dims), mesh=mesh, in_specs=in_specs,
        out_specs=P(tokens, None), check_vma=False,
    )
```
